32 devices in a mesh: tm: 4 (over y, x), space: 8 (over z, core).
Axes of the slice: x: 2, y: 2, z: 4, core: 2. Of those that a mesh axis runs over, the one named last changes fastest.
Arguments:
- frames_in: bfloat16 [32, 512, 1024], P('tm', 'space'), may hold values from -6 to 6
- time_gain: float32 [1024], replicated, may hold values from 0.1 to 1.9
- time_shift: float32 [1024], replicated, may hold values from -4 to 4
- time_query: bfloat16 [1024, 1024], replicated
- time_key: bfloat16 [1024, 1024], replicated
- time_value: bfloat16 [1024, 1024], replicated, may hold values from -0.1875 to 0.1875
- time_out: bfloat16 [1024, 1024], replicated, may hold values from -0.1875 to 0.1875
- space_gain: float32 [1024], replicated, may hold values from 0.1 to 1.9
- space_shift: float32 [1024], replicated, may hold values from -4 to 4
- space_query: bfloat16 [1024, 1024], replicated
- space_key: bfloat16 [1024, 1024], replicated
- space_value: bfloat16 [1024, 1024], replicated, may hold values from -0.1875 to 0.1875
- space_out: bfloat16 [1024, 1024], replicated, may hold values from -0.1875 to 0.1875
Outputs:
- frames_out: bfloat16 [32, 512, 1024], P('tm', 'space')
The draws below stay inside these ranges and needn't reach their ends.
All inputs are finite; a program needn't handle non-finite values.
Results may differ from the reference program's by a relative error of at most 0.03.
Values may be sent and summed in bfloat16 or wider, within the bound.
A program may use at most 192 MiB of HBM per device.

```python
import math
import jax
import jax.numpy as jnp
from jax import lax

D = 1024
HEADS = 16
HEAD_DIM = 64
FRAMES = 32
PATCHES = 512


def paired(key, group, which):
    group_key = jax.random.fold_in(key, group)
    factor = (12.0 / HEAD_DIM ** 0.5) ** 0.5
    base = jnp.clip(jax.random.normal(jax.random.fold_in(group_key, which), (D, D), jnp.float32), -4.0, 4.0)
    return (base * factor * D ** (-0.5)).astype(jnp.bfloat16)


def draw_time_query(key, part):
    return paired(key, 1, 0)


def draw_time_key(key, part):
    return paired(key, 1, 1)


def draw_space_query(key, part):
    return paired(key, 2, 0)


def draw_space_key(key, part):
    return paired(key, 2, 1)


def levels(own_key, extent, split, smallest, largest):
    def one(dim, parts):
        draws = jax.random.uniform(jax.random.fold_in(jax.random.fold_in(own_key, 6), dim), (parts,), jnp.float32, smallest / len(split), largest / len(split))
        return jnp.repeat(jnp.exp(draws), extent[dim] // parts).reshape((-1,) + (1,) * (len(extent) - dim - 1))

    loudness = one(*split[0])
    for cut in split[1:]:
        loudness = loudness * one(*cut)
    return loudness


def centred(stream_key, shape, deviation, most, pieces=(), kind=jnp.bfloat16):
    values = deviation * jax.random.normal(stream_key, shape, jnp.float32)
    if pieces:
        values = values * levels(stream_key, shape, pieces, -0.22, 0.18)
    return jnp.clip(values, -most, most).astype(kind)


def setup_inputs(seed: int = 0) -> dict:
    arg_keys = jax.random.split(jax.random.key(seed), 14)
    frames_in = centred(arg_keys[0], (FRAMES, PATCHES, D), 1.0, 6.0, ((0, 4), (1, 8)))
    time_gain = jnp.clip(1.0 + 0.18 * jax.random.normal(arg_keys[1], (D,), jnp.float32), 0.1, 1.9)
    time_shift = centred(arg_keys[2], (D,), 1.0, 4.0, (), jnp.float32)
    time_query = draw_time_query(jax.random.fold_in(arg_keys[13], 71), 0)
    time_key = draw_time_key(jax.random.fold_in(arg_keys[13], 71), 0)
    time_value = centred(arg_keys[5], (D, D), D ** -0.5, 0.1875)
    time_out = centred(arg_keys[6], (D, D), D ** -0.5, 0.1875)
    space_gain = jnp.clip(1.0 + 0.18 * jax.random.normal(arg_keys[7], (D,), jnp.float32), 0.1, 1.9)
    space_shift = centred(arg_keys[8], (D,), 1.0, 4.0, (), jnp.float32)
    space_query = draw_space_query(jax.random.fold_in(arg_keys[13], 71), 0)
    space_key = draw_space_key(jax.random.fold_in(arg_keys[13], 71), 0)
    space_value = centred(arg_keys[11], (D, D), D ** -0.5, 0.1875)
    space_out = centred(arg_keys[12], (D, D), D ** -0.5, 0.1875)
    return dict(frames_in=frames_in, time_gain=time_gain, time_shift=time_shift, time_query=time_query, time_key=time_key, time_value=time_value, time_out=time_out, space_gain=space_gain, space_shift=space_shift, space_query=space_query, space_key=space_key, space_value=space_value, space_out=space_out)


def layer_norm(tokens, gain, shift):
    values = tokens.astype(jnp.float32)
    mean_value = lax.optimization_barrier(jnp.mean(values, axis=-1, keepdims=True))
    variance = lax.optimization_barrier(jnp.mean((values - mean_value) ** 2, axis=-1, keepdims=True))
    return ((values - mean_value) * lax.rsqrt(variance + 1e-05) * gain + shift).astype(jnp.bfloat16)

def project(tokens, weight):
    return jnp.dot(tokens, weight, preferred_element_type=jnp.float32)

def attend(queries, keys_in, values_in):
    scores = jnp.einsum('bqhd,bkhd->bhqk', queries.astype(jnp.float32), keys_in.astype(jnp.float32)) * 0.125
    weights = jax.nn.softmax(scores, axis=-1).astype(jnp.bfloat16)
    result = jnp.einsum('bhqk,bkhd->bqhd', weights.astype(jnp.float32), values_in.astype(jnp.float32))
    return result.astype(jnp.bfloat16)

def heads_of(tokens):
    return tokens.reshape(FRAMES, PATCHES, HEADS, HEAD_DIM)

def reference(frames_in, time_gain, time_shift, time_query, time_key, time_value, time_out, space_gain, space_shift, space_query, space_key, space_value, space_out):
    normed = layer_norm(frames_in, time_gain, time_shift)
    block_size = math.gcd(PATCHES, 64)
    groups = []
    for weight in (time_query, time_key, time_value):
        heads = heads_of(project(normed, weight).astype(jnp.bfloat16))
        heads = jnp.transpose(heads, (1, 0, 2, 3)).reshape(PATCHES // block_size, block_size, FRAMES, HEADS, HEAD_DIM)
        groups.append(heads)

    def time_block(triple):
        return attend(triple[0], triple[1], triple[2])
    attended = lax.map(time_block, tuple(groups))
    attended = jnp.transpose(attended.reshape(PATCHES, FRAMES, D), (1, 0, 2))
    after_time = (frames_in.astype(jnp.float32) + project(attended, time_out)).astype(jnp.bfloat16)
    normed = layer_norm(after_time, space_gain, space_shift)
    triple = tuple((heads_of(project(normed, weight).astype(jnp.bfloat16)) for weight in (space_query, space_key, space_value)))

    def space_frame(frame_triple):
        return attend(frame_triple[0][None], frame_triple[1][None], frame_triple[2][None])[0]
    spatial = lax.map(space_frame, triple).reshape(FRAMES, PATCHES, D)
    return (after_time.astype(jnp.float32) + project(spatial, space_out)).astype(jnp.bfloat16)
```

```python
import functools
import math

import jax
import jax.numpy as jnp
from jax import lax
from jax.experimental import pallas as pl
from jax.experimental.pallas import tpu as pltpu
from jax.sharding import PartitionSpec as P

HEAD_DIM = 64
LANES = 128
SCALE = 0.125 * math.log2(math.e)
F32, BF16 = jnp.float32, jnp.bfloat16


def layer_norm(tokens, gain, shift):
    values = tokens.astype(F32)
    mean_value = jnp.mean(values, axis=-1, keepdims=True)
    centred = values - mean_value
    variance = jnp.mean(centred * centred, axis=-1, keepdims=True)
    return (centred * lax.rsqrt(variance + 1e-05) * gain + shift).astype(BF16)


def project(tokens, weight):
    return jnp.dot(tokens, weight, preferred_element_type=F32)


def permutation(rows, inner, outer, back):
    row = lax.broadcasted_iota(jnp.int32, (rows, rows), 1 if back else 0)
    col = lax.broadcasted_iota(jnp.int32, (rows, rows), 0 if back else 1)
    return jnp.where((row % inner) * outer + row // inner == col, 1.0, 0.0).astype(BF16)


def lane_masks(width):
    lane = lax.broadcasted_iota(jnp.int32, (1, LANES), 1)
    return [(lane // HEAD_DIM == part) for part in range(LANES // HEAD_DIM)]


def attend(queries, keys_in, values_in, same):
    result = None
    for mask in lane_masks(LANES):
        own = jnp.where(mask, queries, jnp.zeros_like(queries))
        scores = lax.dot_general(
            own, keys_in, (((1,), (1,)), ((), ())), preferred_element_type=F32
        )
        if same is not None:
            scores = jnp.where(same, scores, -1e30)
        top = jnp.max(scores, axis=-1, keepdims=True)
        weights = jnp.exp2((scores - top) * SCALE)
        total = jnp.sum(weights, axis=-1, keepdims=True)
        added = jnp.dot(weights.astype(BF16), values_in, preferred_element_type=F32) / total
        result = added if result is None else jnp.where(mask, added, result)
    return result.astype(BF16)


def qkv(normed, weights, waits, outs):
    for weight, wait, out in zip(weights, waits, outs):
        wait()
        out[...] = project(normed, weight[...]).astype(BF16)


def time_branch(frames, x, gain, shift, weights, waits, q, k, v, a):
    rows, width = q.shape
    places = rows // frames
    order = permutation(rows, frames, places, False)
    x = project(order, x).astype(BF16)
    qkv(layer_norm(x, gain, shift), weights[:3], waits[:3], (q, k, v))
    size = max(frames, LANES)
    same = (
        lax.broadcasted_iota(jnp.int32, (size, size), 0) // frames
        == lax.broadcasted_iota(jnp.int32, (size, size), 1) // frames
    )

    def pair(index, carry):
        cols = pl.ds(pl.multiple_of(index * LANES, LANES), LANES)
        for group in range(rows // size):
            part = (pl.ds(group * size, size), cols)
            a[part] = attend(q[part], k[part], v[part], same)
        return carry

    lax.fori_loop(0, width // LANES, pair, 0)
    waits[3]()
    after = (x.astype(F32) + project(a[...], weights[3][...])).astype(BF16)
    return project(permutation(rows, frames, places, True), after).astype(BF16)


def space_branch(x, gain, shift, weights, waits, q, k, v, a):
    rows, width = q.shape
    qkv(layer_norm(x, gain, shift), weights[:3], waits[:3], (q, k, v))

    def pair(index, carry):
        cols = pl.ds(pl.multiple_of(index * LANES, LANES), LANES)
        a[:, cols] = attend(q[:, cols], k[:, cols], v[:, cols], None)
        return carry

    lax.fori_loop(0, width // LANES, pair, 0)
    waits[3]()
    return (x.astype(F32) + project(a[...], weights[3][...])).astype(BF16)


def branch_kernel(branch, x, gain, shift, w0, w1, w2, w3, out, held, q, k, v, a, sems):
    copies = [
        pltpu.make_async_copy(w, held.at[i], sems.at[i]) for i, w in enumerate((w0, w1, w2, w3))
    ]
    for copy in copies:
        copy.start()
    weights = [held.at[i] for i in range(4)]
    waits = [copy.wait for copy in copies]
    out[...] = branch(x[...], gain[...], shift[...], weights, waits, q, k, v, a)


def run_branch(branch, x, gain, shift, *weights):
    rows, width = x.shape
    vmem = pl.BlockSpec(memory_space=pltpu.VMEM)
    return pl.pallas_call(
        functools.partial(branch_kernel, branch),
        out_shape=jax.ShapeDtypeStruct((rows, width), BF16),
        in_specs=[vmem] * 3 + [pl.BlockSpec(memory_space=pl.ANY)] * 4,
        out_specs=vmem,
        scratch_shapes=[pltpu.VMEM((4, width, width), BF16)]
        + [pltpu.VMEM((rows, width), BF16)] * 4
        + [pltpu.SemaphoreType.DMA((4,))],
        compiler_params=pltpu.CompilerParams(vmem_limit_bytes=60 << 20),
    )(x, gain.reshape(1, -1), shift.reshape(1, -1), *weights)


def split_heads(tokens):
    return tokens.reshape(tokens.shape[0], tokens.shape[1], tokens.shape[2] // HEAD_DIM, HEAD_DIM)


def gathered_space(after_time, gain, shift, wq, wk, wv, wo):
    normed = layer_norm(after_time, gain, shift)
    queries = project(normed, wq).astype(BF16)
    everywhere = lax.all_gather(normed, "space", axis=1, tiled=True)
    keys_in, values_in = (project(everywhere, w).astype(BF16) for w in (wk, wv))
    scores = 0.125 * jnp.einsum(
        "fqhd,fkhd->fhqk", split_heads(queries), split_heads(keys_in), preferred_element_type=F32
    )
    weights = jax.nn.softmax(scores, axis=-1).astype(BF16)
    spatial = jnp.einsum(
        "fhqk,fkhd->fqhd", weights, split_heads(values_in), preferred_element_type=F32
    )
    spatial = spatial.astype(BF16).reshape(after_time.shape)
    return (after_time.astype(F32) + project(spatial, wo)).astype(BF16)


def body(frames_in, tg, ts, tq, tk, tv, to, sg, ss, sq, sk, sv, so):
    slots, spread = lax.axis_size("tm"), lax.axis_size("space")
    rows, patches, width = frames_in.shape
    frames, places = rows * slots, patches // slots
    tokens = lax.all_to_all(
        frames_in.reshape(rows, slots, places, width), "tm", split_axis=1, concat_axis=0, tiled=True
    ).reshape(frames * places, width)
    after = run_branch(functools.partial(time_branch, frames), tokens, tg, ts, tq, tk, tv, to)
    if rows != spread:
        after = lax.all_to_all(
            after.reshape(frames, 1, places, width), "tm", split_axis=0, concat_axis=1, tiled=True
        ).reshape(rows, patches, width)
        return gathered_space(after, sg, ss, sq, sk, sv, so)
    frame = lax.all_to_all(
        after.reshape(frames, places, width), ("tm", "space"), split_axis=0, concat_axis=0, tiled=True
    ).reshape(frames * places, width)
    done = run_branch(space_branch, frame, sg, ss, sq, sk, sv, so)
    done = done.reshape(slots, spread, places, width).transpose(1, 0, 2, 3)
    return lax.all_to_all(done, "space", split_axis=0, concat_axis=0, tiled=True).reshape(
        rows, patches, width
    )


def solution(mesh):
    return jax.shard_map(
        body,
        mesh=mesh,
        in_specs=(P("tm", "space", None),) + (P(),) * 12,
        out_specs=P("tm", "space", None),
        check_vma=False,
    )
```

```python
import functools
import math

import jax
import jax.numpy as jnp
from jax import lax
from jax.experimental import pallas as pl
from jax.experimental.pallas import tpu as pltpu
from jax.sharding import PartitionSpec as P

HEAD_DIM = 64
LANES = 128
SCALE = 0.125 * math.log2(math.e)
F32, BF16 = jnp.float32, jnp.bfloat16


def layer_norm(tokens, gain, shift):
    values = tokens.astype(F32)
    mean_value = jnp.mean(values, axis=-1, keepdims=True)
    centred = values - mean_value
    variance = jnp.mean(centred * centred, axis=-1, keepdims=True)
    return (centred * lax.rsqrt(variance + 1e-05) * gain + shift).astype(BF16)


def project(tokens, weight):
    return jnp.dot(tokens, weight, preferred_element_type=F32)


def permutation(rows, inner, outer, back):
    row = lax.broadcasted_iota(jnp.int32, (rows, rows), 1 if back else 0)
    col = lax.broadcasted_iota(jnp.int32, (rows, rows), 0 if back else 1)
    return jnp.where((row % inner) * outer + row // inner == col, 1.0, 0.0).astype(BF16)


def lane_masks(width):
    lane = lax.broadcasted_iota(jnp.int32, (1, LANES), 1)
    return [(lane // HEAD_DIM == part) for part in range(LANES // HEAD_DIM)]


def attend(queries, keys_in, values_in, same):
    rows = queries.shape[0]
    masks = lane_masks(LANES)
    own = jnp.concatenate([jnp.where(mask, queries, jnp.zeros_like(queries)) for mask in masks], 0)
    scores = lax.dot_general(own, keys_in, (((1,), (1,)), ((), ())), preferred_element_type=F32)
    if same is not None:
        scores = jnp.where(jnp.concatenate([same] * len(masks), 0), scores, -1e30)
    top = jnp.max(scores, axis=-1, keepdims=True)
    weights = jnp.exp2((scores - top) * SCALE).astype(BF16)
    both = jnp.concatenate([values_in, jnp.ones_like(values_in)], 1)
    added = jnp.dot(weights, both, preferred_element_type=F32)
    added = added[:, :LANES] / added[:, LANES:]
    result = added[:rows]
    for part in range(1, len(masks)):
        result = jnp.where(masks[part], added[part * rows : (part + 1) * rows], result)
    return result.astype(BF16)


def qkv(normed, weights, waits, outs):
    for weight, wait, out in zip(weights, waits, outs):
        wait()
        out[...] = project(normed, weight[...]).astype(BF16)


def time_branch(frames, x, gain, shift, weights, waits, q, k, v, a):
    rows, width = q.shape
    places = rows // frames
    order = permutation(rows, frames, places, False)
    x = project(order, x).astype(BF16)
    qkv(layer_norm(x, gain, shift), weights[:3], waits[:3], (q, k, v))
    size = max(frames, LANES)
    same = (
        lax.broadcasted_iota(jnp.int32, (size, size), 0) // frames
        == lax.broadcasted_iota(jnp.int32, (size, size), 1) // frames
    )

    def pair(index, carry):
        cols = pl.ds(pl.multiple_of(index * LANES, LANES), LANES)
        for group in range(rows // size):
            part = (pl.ds(group * size, size), cols)
            a[part] = attend(q[part], k[part], v[part], same)
        return carry

    lax.fori_loop(0, width // LANES, pair, 0, unroll=2)
    waits[3]()
    after = (x.astype(F32) + project(a[...], weights[3][...])).astype(BF16)
    return project(permutation(rows, frames, places, True), after)


def branch_kernel(branch, x, gain, shift, w0, w1, w2, w3, out, held, q, k, v, a, sems):
    copies = [
        pltpu.make_async_copy(w, held.at[i], sems.at[i]) for i, w in enumerate((w0, w1, w2, w3))
    ]
    for copy in copies:
        copy.start()
    weights = [held.at[i] for i in range(4)]
    waits = [copy.wait for copy in copies]
    out[...] = branch(x[...], gain[...], shift[...], weights, waits, q, k, v, a).astype(BF16)


def run_branch(branch, x, gain, shift, *weights):
    rows, width = x.shape
    vmem = pl.BlockSpec(memory_space=pltpu.VMEM)
    return pl.pallas_call(
        functools.partial(branch_kernel, branch),
        out_shape=jax.ShapeDtypeStruct((rows, width), BF16),
        in_specs=[vmem] * 3 + [pl.BlockSpec(memory_space=pl.ANY)] * 4,
        out_specs=vmem,
        scratch_shapes=[pltpu.VMEM((4, width, width), BF16)]
        + [pltpu.VMEM((rows, width), BF16)] * 4
        + [pltpu.SemaphoreType.DMA((4,))],
        compiler_params=pltpu.CompilerParams(vmem_limit_bytes=60 << 20),
    )(x, gain.reshape(1, -1), shift.reshape(1, -1), *weights)


def flipped(index, mask):
    result, bit = index + mask, 1
    while bit < 64:
        result = result - 2 * bit * ((index // bit) % 2) * ((mask // bit) % 2)
        bit *= 2
    return result


def layer_kernel(
    slots,
    spread,
    x,
    tg,
    ts,
    sg,
    ss,
    *refs,
):
    sources, out = refs[:8], refs[8]
    held, xt, snd, rcv, done, q, k, v, a, wsem, lsem, s1, r1, s2, r2, s3, r3 = refs[9:]
    me_t, me_s = lax.axis_index("tm"), lax.axis_index("space")
    frames, piece, width = xt.shape[1:]
    rows, halves = frames // slots, xt.shape[0]
    peers = slots * spread
    tokens = frames * piece

    def device(mask):
        return flipped(me_t, mask % slots), flipped(me_s, mask // slots)

    barrier = pltpu.get_barrier_semaphore()

    def greet(n, carry):
        t, s = device(n + 1)
        pl.semaphore_signal(barrier, inc=1, device_id={"tm": t, "space": s})
        return carry

    lax.fori_loop(0, peers - 1, greet, 0)
    loads = [pltpu.make_async_copy(w, held.at[i], wsem.at[i]) for i, w in enumerate(sources)]
    locals_in = [
        pltpu.make_async_copy(
            x.at[:, me_t, h], xt.at[h, pl.ds(me_t * rows, rows)], lsem.at[h]
        )
        for h in range(halves)
    ]
    for copy in locals_in + loads:
        copy.start()
    pl.semaphore_wait(barrier, peers - 1)

    def first(h, mask):
        t = flipped(me_t, mask)
        return pltpu.make_async_remote_copy(
            src_ref=x.at[:, t, h],
            dst_ref=xt.at[h, pl.ds(me_t * rows, rows)],
            send_sem=s1.at[h, mask],
            recv_sem=r1.at[h, mask],
            device_id={"tm": t},
        )

    def second(h, mask):
        t, s = device(mask)
        return pltpu.make_async_remote_copy(
            src_ref=snd.at[h, t * rows + s],
            dst_ref=rcv.at[(me_s * slots + me_t) * halves + h],
            send_sem=s2.at[h, mask],
            recv_sem=r2.at[h, mask],
            device_id={"tm": t, "space": s},
        )

    for h in range(halves):
        for mask in range(slots - 1, 0, -1):
            first(h, mask).start()

    weights = [held.at[i] for i in range(8)]
    waits = [copy.wait for copy in loads]
    for h in range(halves):
        locals_in[h].wait()
        for mask in range(1, slots):
            first(h, mask).wait_recv()
        part = [ref.at[pl.ds(0, tokens)] for ref in (q, k, v, a)]
        after = time_branch(
            frames,
            xt[h].astype(F32).reshape(tokens, width).astype(BF16),
            tg[...],
            ts[...],
            weights[:4],
            waits[:4] if h == 0 else [lambda: None] * 4,
            *part,
        )
        after = after.reshape(frames, piece, width).astype(BF16)
        snd[h] = after

        def send(n, carry):
            second(h, peers - 1 - n).start()
            return carry

        lax.fori_loop(0, peers - 1, send, 0)
        rcv[(me_s * slots + me_t) * halves + h] = snd[h, me_t * rows + me_s]

    def arrive(n, carry):
        for h in range(halves):
            second(h, peers - 1 - n).wait_recv()
        return carry

    lax.fori_loop(0, peers - 1, arrive, 0)
    total = q.shape[0]
    frame = rcv[...].astype(F32).reshape(total, width).astype(BF16)
    done[...] = frame
    qkv(layer_norm(frame, sg[...], ss[...]), weights[4:7], waits[4:7], (q, k, v))
    waits[7]()
    share = total // spread
    group = 2 if spread % 2 == 0 else 1
    steps = spread // group

    def third(mask):
        s = flipped(me_s, mask)
        return pltpu.make_async_remote_copy(
            src_ref=done.at[pl.ds(pl.multiple_of(s * share, share), share)],
            dst_ref=out.at[me_s],
            send_sem=s3.at[mask],
            recv_sem=r3.at[mask],
            device_id={"space": s},
        )

    for step in range(steps - 1, -1, -1):
        size = group * share
        chunk = pl.ds(pl.multiple_of(flipped(me_s // group, step) * size, size), size)

        def pair(index, carry):
            cols = pl.ds(pl.multiple_of(index * LANES, LANES), LANES)
            a[chunk, cols] = attend(q[chunk, cols], k[:, cols], v[:, cols], None)
            return carry

        lax.fori_loop(0, width // LANES, pair, 0, unroll=2)
        done[chunk] = (done[chunk].astype(F32) + project(a[chunk], weights[7][...])).astype(BF16)
        for member in range(group - 1, -1, -1):
            if step * group + member:
                third(step * group + member).start()
    last = pltpu.make_async_copy(
        done.at[pl.ds(pl.multiple_of(me_s * share, share), share)], out.at[me_s], lsem.at[0]
    )
    last.start()
    for h in range(halves):
        for mask in range(1, slots):
            first(h, mask).wait_send()

    def left(n, carry):
        for h in range(halves):
            second(h, n + 1).wait_send()
        return carry

    lax.fori_loop(0, peers - 1, left, 0)
    for mask in range(1, spread):
        third(mask).wait()
    last.wait()


def run_layer(frames_in, slots, spread, norms, weights):
    rows, patches, width = frames_in.shape
    frames, places, halves = rows * slots, patches // slots, 2
    piece = places // halves
    total = frames * places
    vmem, hbm = pl.BlockSpec(memory_space=pltpu.VMEM), pl.BlockSpec(memory_space=pl.ANY)
    dma = pltpu.SemaphoreType.DMA
    return pl.pallas_call(
        functools.partial(layer_kernel, slots, spread),
        out_shape=jax.ShapeDtypeStruct(frames_in.shape, BF16),
        in_specs=[hbm] + [vmem] * 4 + [hbm] * 8,
        out_specs=hbm,
        scratch_shapes=[
            pltpu.VMEM((8, width, width), BF16),
            pltpu.VMEM((halves, frames, piece, width), BF16),
            pltpu.VMEM((halves, frames, piece, width), BF16),
            pltpu.VMEM((total // piece, piece, width), BF16),
        ]
        + [pltpu.VMEM((total, width), BF16)] * 5
        + [
            dma((8,)),
            dma((halves,)),
            dma((halves, slots)),
            dma((halves, slots)),
            dma((halves, slots * spread)),
            dma((halves, slots * spread)),
            dma((spread,)),
            dma((spread,)),
        ],
        compiler_params=pltpu.CompilerParams(
            collective_id=0, has_side_effects=True, vmem_limit_bytes=60 << 20
        ),
    )(
        frames_in.reshape(rows, slots, halves, piece, width),
        *[norm.reshape(1, -1) for norm in norms],
        *weights,
    )


def split_heads(tokens):
    return tokens.reshape(tokens.shape[0], tokens.shape[1], tokens.shape[2] // HEAD_DIM, HEAD_DIM)


def gathered_space(after_time, gain, shift, wq, wk, wv, wo):
    normed = layer_norm(after_time, gain, shift)
    queries = project(normed, wq).astype(BF16)
    everywhere = lax.all_gather(normed, "space", axis=1, tiled=True)
    keys_in, values_in = (project(everywhere, w).astype(BF16) for w in (wk, wv))
    scores = 0.125 * jnp.einsum(
        "fqhd,fkhd->fhqk", split_heads(queries), split_heads(keys_in), preferred_element_type=F32
    )
    weights = jax.nn.softmax(scores, axis=-1).astype(BF16)
    spatial = jnp.einsum(
        "fhqk,fkhd->fqhd", weights, split_heads(values_in), preferred_element_type=F32
    )
    spatial = spatial.astype(BF16).reshape(after_time.shape)
    return (after_time.astype(F32) + project(spatial, wo)).astype(BF16)


def body(frames_in, tg, ts, tq, tk, tv, to, sg, ss, sq, sk, sv, so):
    slots, spread = lax.axis_size("tm"), lax.axis_size("space")
    rows, patches, width = frames_in.shape
    frames, places = rows * slots, patches // slots
    if rows == spread and not (slots & (slots - 1) or spread & (spread - 1)):
        return run_layer(
            frames_in, slots, spread, (tg, ts, sg, ss), (tq, tk, tv, to, sq, sk, sv, so)
        )
    tokens = lax.all_to_all(
        frames_in.reshape(rows, slots, places, width), "tm", split_axis=1, concat_axis=0, tiled=True
    ).reshape(frames * places, width)
    after = run_branch(functools.partial(time_branch, frames), tokens, tg, ts, tq, tk, tv, to)
    after = lax.all_to_all(
        after.reshape(frames, 1, places, width), "tm", split_axis=0, concat_axis=1, tiled=True
    ).reshape(rows, patches, width)
    return gathered_space(after, sg, ss, sq, sk, sv, so)


def solution(mesh):
    return jax.shard_map(
        body,
        mesh=mesh,
        in_specs=(P("tm", "space", None),) + (P(),) * 12,
        out_specs=P("tm", "space", None),
        check_vma=False,
    )
```

```python
import functools
import math

import jax
import jax.numpy as jnp
from jax import lax
from jax.experimental import pallas as pl
from jax.experimental.pallas import tpu as pltpu
from jax.sharding import PartitionSpec as P

HEAD_DIM = 64
LANES = 128
SCALE = 0.125 * math.log2(math.e)
F32, BF16 = jnp.float32, jnp.bfloat16


def layer_norm(tokens, gain, shift):
    values = tokens.astype(F32)
    mean_value = jnp.mean(values, axis=-1, keepdims=True)
    centred = values - mean_value
    variance = jnp.mean(centred * centred, axis=-1, keepdims=True)
    return (centred * lax.rsqrt(variance + 1e-05) * gain + shift).astype(BF16)


def project(tokens, weight):
    return jnp.dot(tokens, weight, preferred_element_type=F32)


def permutation(rows, inner, outer, back):
    row = lax.broadcasted_iota(jnp.int32, (rows, rows), 1 if back else 0)
    col = lax.broadcasted_iota(jnp.int32, (rows, rows), 0 if back else 1)
    return jnp.where((row % inner) * outer + row // inner == col, 1.0, 0.0).astype(BF16)


def lane_masks(width):
    lane = lax.broadcasted_iota(jnp.int32, (1, LANES), 1)
    return [(lane // HEAD_DIM == part) for part in range(LANES // HEAD_DIM)]


def attend(queries, keys_in, values_in, same):
    rows = queries.shape[0]
    masks = lane_masks(LANES)
    own = jnp.concatenate([jnp.where(mask, queries, jnp.zeros_like(queries)) for mask in masks], 0)
    scores = lax.dot_general(own, keys_in, (((1,), (1,)), ((), ())), preferred_element_type=F32)
    if same is not None:
        scores = jnp.where(jnp.concatenate([same] * len(masks), 0), scores, -1e30)
    top = jnp.max(scores, axis=-1, keepdims=True)
    weights = jnp.exp2((scores - top) * SCALE).astype(BF16)
    both = jnp.concatenate([values_in, jnp.ones_like(values_in)], 1)
    added = jnp.dot(weights, both, preferred_element_type=F32)
    added = added[:, :LANES] / added[:, LANES:]
    result = added[:rows]
    for part in range(1, len(masks)):
        result = jnp.where(masks[part], added[part * rows : (part + 1) * rows], result)
    return result.astype(BF16)


def qkv(normed, weights, waits, outs):
    for weight, wait, out in zip(weights, waits, outs):
        wait()
        out[...] = project(normed, weight[...]).astype(BF16)


def time_branch(frames, x, gain, shift, weights, waits, q, k, v, a):
    rows, width = q.shape
    places = rows // frames
    order = permutation(rows, frames, places, False)
    x = project(order, x).astype(BF16)
    qkv(layer_norm(x, gain, shift), weights[:3], waits[:3], (q, k, v))
    size = max(frames, LANES)
    same = (
        lax.broadcasted_iota(jnp.int32, (size, size), 0) // frames
        == lax.broadcasted_iota(jnp.int32, (size, size), 1) // frames
    )

    def pair(index, carry):
        cols = pl.ds(pl.multiple_of(index * LANES, LANES), LANES)
        for group in range(rows // size):
            part = (pl.ds(group * size, size), cols)
            a[part] = attend(q[part], k[part], v[part], same)
        return carry

    lax.fori_loop(0, width // LANES, pair, 0, unroll=2)
    waits[3]()
    after = (x.astype(F32) + project(a[...], weights[3][...])).astype(BF16)
    return project(permutation(rows, frames, places, True), after)


def branch_kernel(branch, x, gain, shift, w0, w1, w2, w3, out, held, q, k, v, a, sems):
    copies = [
        pltpu.make_async_copy(w, held.at[i], sems.at[i]) for i, w in enumerate((w0, w1, w2, w3))
    ]
    for copy in copies:
        copy.start()
    weights = [held.at[i] for i in range(4)]
    waits = [copy.wait for copy in copies]
    out[...] = branch(x[...], gain[...], shift[...], weights, waits, q, k, v, a).astype(BF16)


def run_branch(branch, x, gain, shift, *weights):
    rows, width = x.shape
    vmem = pl.BlockSpec(memory_space=pltpu.VMEM)
    return pl.pallas_call(
        functools.partial(branch_kernel, branch),
        out_shape=jax.ShapeDtypeStruct((rows, width), BF16),
        in_specs=[vmem] * 3 + [pl.BlockSpec(memory_space=pl.ANY)] * 4,
        out_specs=vmem,
        scratch_shapes=[pltpu.VMEM((4, width, width), BF16)]
        + [pltpu.VMEM((rows, width), BF16)] * 4
        + [pltpu.SemaphoreType.DMA((4,))],
        compiler_params=pltpu.CompilerParams(vmem_limit_bytes=60 << 20),
    )(x, gain.reshape(1, -1), shift.reshape(1, -1), *weights)


def flipped(index, mask):
    result, bit = index + mask, 1
    while bit < 64:
        result = result - 2 * bit * ((index // bit) % 2) * ((mask // bit) % 2)
        bit *= 2
    return result


def layer_kernel(
    slots,
    spread,
    x,
    tg,
    ts,
    sg,
    ss,
    *refs,
):
    sources, out = refs[:8], refs[8]
    held, xt, snd, rcv, q, k, v, a, wsem, lsem, s1, r1, s2, r2, s3, r3 = refs[9:]
    me_t, me_s = lax.axis_index("tm"), lax.axis_index("space")
    frames, piece, width = xt.shape[1:]
    rows, halves = frames // slots, xt.shape[0]
    peers = slots * spread
    tokens = frames * piece

    def device(mask):
        return flipped(me_t, mask % slots), flipped(me_s, mask // slots)

    barrier = pltpu.get_barrier_semaphore()

    def greet(n, carry):
        t, s = device(n + 1)
        pl.semaphore_signal(barrier, inc=1, device_id={"tm": t, "space": s})
        return carry

    lax.fori_loop(0, peers - 1, greet, 0)
    loads = [pltpu.make_async_copy(w, held.at[i], wsem.at[i]) for i, w in enumerate(sources)]
    locals_in = [
        pltpu.make_async_copy(
            x.at[:, me_t, h], xt.at[h, pl.ds(me_t * rows, rows)], lsem.at[h]
        )
        for h in range(halves)
    ]
    for copy in locals_in + loads:
        copy.start()
    pl.semaphore_wait(barrier, peers - 1)

    def first(h, mask):
        t = flipped(me_t, mask)
        return pltpu.make_async_remote_copy(
            src_ref=x.at[:, t, h],
            dst_ref=xt.at[h, pl.ds(me_t * rows, rows)],
            send_sem=s1.at[h, mask],
            recv_sem=r1.at[h, mask],
            device_id={"tm": t},
        )

    def second(h, mask):
        t, s = device(mask)
        return pltpu.make_async_remote_copy(
            src_ref=snd.at[h, t * rows + s],
            dst_ref=rcv.at[h * peers + me_s * slots + me_t],
            send_sem=s2.at[h, mask],
            recv_sem=r2.at[h, mask],
            device_id={"tm": t, "space": s},
        )

    for h in range(halves):
        for mask in range(slots - 1, 0, -1):
            first(h, mask).start()

    weights = [held.at[i] for i in range(8)]
    waits = [copy.wait for copy in loads]
    for h in range(halves):
        locals_in[h].wait()
        for mask in range(1, slots):
            first(h, mask).wait_recv()
        part = [ref.at[pl.ds(0, tokens)] for ref in (q, k, v, a)]
        after = time_branch(
            frames,
            xt[h].astype(F32).reshape(tokens, width).astype(BF16),
            tg[...],
            ts[...],
            weights[:4],
            waits[:4] if h == 0 else [lambda: None] * 4,
            *part,
        )
        after = after.reshape(frames, piece, width).astype(BF16)
        snd[h] = after

        def send(n, carry):
            second(h, peers - 1 - n).start()
            return carry

        lax.fori_loop(0, peers - 1, send, 0)
        rcv[h * peers + me_s * slots + me_t] = snd[h, me_t * rows + me_s]

    for h in range(halves):

        def arrive(n, carry):
            second(h, peers - 1 - n).wait_recv()
            return carry

        lax.fori_loop(0, peers - 1, arrive, 0)
        frame = rcv[pl.ds(h * peers, peers)].astype(F32).reshape(tokens, width).astype(BF16)
        qkv(
            layer_norm(frame, sg[...], ss[...]),
            weights[4:7],
            waits[4:7] if h == 0 else [lambda: None] * 3,
            [ref.at[pl.ds(h * tokens, tokens)] for ref in (q, k, v)],
        )
    waits[7]()
    share = slots * piece
    group = 2 if spread % 2 == 0 else 1
    steps = spread // group

    def blocks(h, s, count):
        return pl.ds(h * peers + s * slots, count * slots)

    def third(h, mask):
        s = flipped(me_s, mask)
        return pltpu.make_async_remote_copy(
            src_ref=rcv.at[blocks(h, s, 1)],
            dst_ref=out.at[me_s, :, h],
            send_sem=s3.at[h, mask],
            recv_sem=r3.at[h, mask],
            device_id={"space": s},
        )

    for step in range(steps - 1, -1, -1):
        size = group * share
        base = flipped(me_s // group, step) * group
        parts = [
            pl.ds(pl.multiple_of(h * tokens + base * share, size), size) for h in range(halves)
        ]

        def pair(index, carry):
            cols = pl.ds(pl.multiple_of(index * LANES, LANES), LANES)
            queries = jnp.concatenate([q[part, cols] for part in parts], 0)
            result = attend(queries, k[:, cols], v[:, cols], None)
            for h, part in enumerate(parts):
                a[part, cols] = result[h * size : (h + 1) * size]
            return carry

        lax.fori_loop(0, width // LANES, pair, 0, unroll=2)
        added = project(jnp.concatenate([a[part] for part in parts], 0), weights[7][...])
        for h in range(halves):
            here = blocks(h, base, group)
            new = added[h * size : (h + 1) * size].reshape(group * slots, piece, width)
            rcv[here] = (rcv[here].astype(F32) + new).astype(BF16)
        for member in range(group - 1, -1, -1):
            if step * group + member:
                for h in range(halves):
                    third(h, step * group + member).start()
    last = [
        pltpu.make_async_copy(rcv.at[blocks(h, me_s, 1)], out.at[me_s, :, h], lsem.at[h])
        for h in range(halves)
    ]
    for copy in last:
        copy.start()
    for h in range(halves):
        for mask in range(1, slots):
            first(h, mask).wait_send()

    def left(n, carry):
        for h in range(halves):
            second(h, n + 1).wait_send()
        return carry

    lax.fori_loop(0, peers - 1, left, 0)
    for h in range(halves):
        for mask in range(1, spread):
            third(h, mask).wait()
        last[h].wait()


def run_layer(frames_in, slots, spread, norms, weights):
    rows, patches, width = frames_in.shape
    frames, places, halves = rows * slots, patches // slots, 2
    piece = places // halves
    total = frames * places
    vmem, hbm = pl.BlockSpec(memory_space=pltpu.VMEM), pl.BlockSpec(memory_space=pltpu.HBM)
    dma = pltpu.SemaphoreType.DMA
    return pl.pallas_call(
        functools.partial(layer_kernel, slots, spread),
        out_shape=jax.ShapeDtypeStruct((rows, slots, halves, piece, width), BF16),
        in_specs=[hbm] + [vmem] * 4 + [hbm] * 8,
        out_specs=hbm,
        scratch_shapes=[
            pltpu.VMEM((8, width, width), BF16),
            pltpu.VMEM((halves, frames, piece, width), BF16),
            pltpu.VMEM((halves, frames, piece, width), BF16),
            pltpu.VMEM((total // piece, piece, width), BF16),
        ]
        + [pltpu.VMEM((total, width), BF16)] * 4
        + [
            dma((8,)),
            dma((halves,)),
            dma((halves, slots)),
            dma((halves, slots)),
            dma((halves, slots * spread)),
            dma((halves, slots * spread)),
            dma((halves, spread)),
            dma((halves, spread)),
        ],
        compiler_params=pltpu.CompilerParams(
            collective_id=0, has_side_effects=True, vmem_limit_bytes=60 << 20
        ),
    )(
        frames_in.reshape(rows, slots, halves, piece, width),
        *[norm.reshape(1, -1) for norm in norms],
        *weights,
    ).reshape(frames_in.shape)


def split_heads(tokens):
    return tokens.reshape(tokens.shape[0], tokens.shape[1], tokens.shape[2] // HEAD_DIM, HEAD_DIM)


def gathered_space(after_time, gain, shift, wq, wk, wv, wo):
    normed = layer_norm(after_time, gain, shift)
    queries = project(normed, wq).astype(BF16)
    everywhere = lax.all_gather(normed, "space", axis=1, tiled=True)
    keys_in, values_in = (project(everywhere, w).astype(BF16) for w in (wk, wv))
    scores = 0.125 * jnp.einsum(
        "fqhd,fkhd->fhqk", split_heads(queries), split_heads(keys_in), preferred_element_type=F32
    )
    weights = jax.nn.softmax(scores, axis=-1).astype(BF16)
    spatial = jnp.einsum(
        "fhqk,fkhd->fqhd", weights, split_heads(values_in), preferred_element_type=F32
    )
    spatial = spatial.astype(BF16).reshape(after_time.shape)
    return (after_time.astype(F32) + project(spatial, wo)).astype(BF16)


def body(frames_in, tg, ts, tq, tk, tv, to, sg, ss, sq, sk, sv, so):
    slots, spread = lax.axis_size("tm"), lax.axis_size("space")
    rows, patches, width = frames_in.shape
    frames, places = rows * slots, patches // slots
    if rows == spread and not (slots & (slots - 1) or spread & (spread - 1)):
        return run_layer(
            frames_in, slots, spread, (tg, ts, sg, ss), (tq, tk, tv, to, sq, sk, sv, so)
        )
    tokens = lax.all_to_all(
        frames_in.reshape(rows, slots, places, width), "tm", split_axis=1, concat_axis=0, tiled=True
    ).reshape(frames * places, width)
    after = run_branch(functools.partial(time_branch, frames), tokens, tg, ts, tq, tk, tv, to)
    after = lax.all_to_all(
        after.reshape(frames, 1, places, width), "tm", split_axis=0, concat_axis=1, tiled=True
    ).reshape(rows, patches, width)
    return gathered_space(after, sg, ss, sq, sk, sv, so)


def solution(mesh):
    return jax.shard_map(
        body,
        mesh=mesh,
        in_specs=(P("tm", "space", None),) + (P(),) * 12,
        out_specs=P("tm", "space", None),
        check_vma=False,
    )
```
